32 devices in a mesh: leaf: 4 (over y, core), panel: 8 (over z, x).
Axes of the slice: x: 2, y: 2, z: 4, core: 2. Of those that a mesh axis runs over, the one named last changes fastest.
Arguments:
- pivot_rhs: float32 [4, 48, 4096], P('leaf', None, 'panel'), may hold values from -6 to 6
- subtree_update: float32 [4, 64, 4096], P('leaf', None, 'panel'), may hold values from -6 to 6
- lower_pivot: bfloat16 [2, 4, 4096, 4096], P(None, 'leaf', 'panel'), as said below
- lower_update: bfloat16 [2, 4, 4096, 4096], P(None, 'leaf', None, 'panel'), as said below
- row_map: int32 [2, 4, 2, 4096], P(None, 'leaf', None, 'panel'), may hold values from 0 to 1023, as said below
- root_inverse: bfloat16 [4096, 4096], P('panel'), as said below
Outputs:
- pivot_solution: float32 [4, 48, 4096], P('leaf', None, 'panel')
- subtree_solution: float32 [4, 64, 4096], P('leaf', None, 'panel')
The draws below stay inside these ranges and needn't reach their ends.
Inputs may be any that keep to these rules, and one draw needn't show every extreme that they name: row_map[l, i] is the same for all i that share i >> (l + 1); within one panel block of 512 rows of one child the values are distinct. lower_pivot[l, i] is the same for all i that share i >> (l + 1), and is zero above its diagonal blocks of 512 rows. lower_update[l, i] is the same for all i that share i >> (l + 1). root_inverse is symmetric.
All inputs are finite; a program needn't handle non-finite values.
Results may differ from the reference program's by a relative error of at most 0.0003.
Values sent between devices are 32-bit elements; how exact they have to be, the bound alone decides.
A program may use at most 64 MiB of HBM per device.

```python
import math
import jax
import jax.numpy as jnp
from jax import lax

VECS = 64
PIV = 4096
UPD = 4096
LEVELS = 2
PBLK = 512
UBLK = 512
OUTCOLS = 48
N_LEAF = 4
N_PANEL = 8


def draw_noise(key, shape):
    return jax.random.normal(key, shape, jnp.float32)


def draw_lower_pivot(key, part):
    block_ids = jnp.arange(PIV) // PBLK
    below_diag = block_ids[:, None] > block_ids[None, :]
    same_block = block_ids[:, None] == block_ids[None, :]
    per_level = []
    for tree_level in range(LEVELS):
        repeat_count = 2 ** (tree_level + 1)
        front_count = N_LEAF // repeat_count
        key_strict, key_inner = jax.random.split(jax.random.fold_in(key, 11 + tree_level))
        strict_part = draw_noise(key_strict, (front_count, PIV, PIV)) * (0.5 / math.sqrt(PIV))
        inner_part = draw_noise(key_inner, (front_count, PIV, PIV)) * (0.3 / math.sqrt(PBLK)) + 0.8 * jnp.eye(PIV, dtype=jnp.float32)
        whole_block = jnp.where(below_diag, strict_part, jnp.where(same_block, inner_part, 0.0)).astype(jnp.bfloat16)
        per_level.append(jnp.repeat(whole_block, repeat_count, axis=0))
    return jnp.stack(per_level)


def draw_lower_update(key, part):
    per_level = []
    for tree_level in range(LEVELS):
        repeat_count = 2 ** (tree_level + 1)
        front_count = N_LEAF // repeat_count
        values = draw_noise(jax.random.fold_in(key, 21 + tree_level), (front_count, UPD, PIV)) * (0.5 / math.sqrt(PIV))
        per_level.append(jnp.repeat(values.astype(jnp.bfloat16), repeat_count, axis=0))
    return jnp.stack(per_level)


def draw_row_map(key, part):
    slot_count = PBLK + UBLK
    per_level = []
    for tree_level in range(LEVELS):
        repeat_count = 2 ** (tree_level + 1)
        front_count = N_LEAF // repeat_count
        scores = jax.random.randint(jax.random.fold_in(key, 31 + tree_level), (front_count, 2, N_PANEL, slot_count), 0, 2 ** 19, dtype=jnp.int32)
        scores = scores * 2048 + jnp.arange(slot_count, dtype=jnp.int32)
        chosen = jnp.argsort(scores, axis=-1)[..., :UBLK].astype(jnp.int32)
        chosen = chosen.reshape(front_count, 2, UPD)
        per_level.append(jnp.repeat(chosen, repeat_count, axis=0))
    return jnp.stack(per_level)


def draw_root_inverse(key, part):
    base_values = draw_noise(key, (UPD, UPD)) * (0.8 / math.sqrt(UPD))
    symmetric = 0.5 * (base_values + base_values.T) + 0.8 * jnp.eye(UPD, dtype=jnp.float32)
    return symmetric.astype(jnp.bfloat16)


def level_of(rng, dims, cuts, least, high):
    level = 1.0
    for axis_at, shards_of in cuts:
        draws = jax.random.uniform(jax.random.fold_in(jax.random.fold_in(rng, 6), axis_at), (shards_of,), jnp.float32, least / len(cuts), high / len(cuts))
        level = level * jnp.repeat(jnp.exp(draws), dims[axis_at] // shards_of).reshape((-1,) + (1,) * (len(dims) - 1 - axis_at))
    return level


def noise(own_key, shape, width, limit, shards=(), kind=jnp.bfloat16):
    drawn = width * jax.random.normal(own_key, shape, jnp.float32)
    if shards:
        drawn = drawn * level_of(own_key, shape, shards, -0.22, 0.18)
    return jnp.clip(drawn, -limit, limit).astype(kind)


def setup_inputs(seed: int = 0) -> dict:
    splits = jax.random.split(jax.random.key(seed), 7)
    return {
        "pivot_rhs": noise(splits[0], (N_LEAF, OUTCOLS, PIV), 1.0, 6.0, ((0, 4), (2, 8)), jnp.float32),
        "subtree_update": noise(splits[1], (N_LEAF, VECS, UPD), 1.0, 6.0, ((0, 4), (2, 8)), jnp.float32),
        "lower_pivot": draw_lower_pivot(jax.random.fold_in(splits[6], 71), 0),
        "lower_update": draw_lower_update(jax.random.fold_in(splits[6], 71), 0),
        "row_map": draw_row_map(jax.random.fold_in(splits[6], 71), 0),
        "root_inverse": draw_root_inverse(jax.random.fold_in(splits[6], 71), 0),
    }


HIGHEST_PRECISION = lax.Precision.HIGHEST


def front_rhs(pivot_rhs, tree_level):
    spread = 2 ** tree_level
    col_count = VECS // spread
    offset = VECS - 2 * col_count
    piece = pivot_rhs[:, offset:offset + col_count, :].reshape(N_LEAF // spread, spread, col_count, PIV)
    return jnp.transpose(piece, (0, 2, 1, 3)).reshape(N_LEAF // spread, VECS, PIV)


def leaf_layout(solution, tree_level):
    spread = 2 ** tree_level
    col_count = VECS // spread
    piece = solution.reshape(N_LEAF // spread, col_count, spread, PIV)
    return jnp.transpose(piece, (0, 2, 1, 3)).reshape(N_LEAF, col_count, PIV)


def front_targets(maps):
    block_ids = (jnp.arange(UPD) // UBLK).astype(jnp.int32)
    pivot_target = block_ids * PBLK + maps
    update_target = PIV + block_ids * UBLK + maps - PBLK
    return jnp.where(maps < PBLK, pivot_target, update_target).astype(jnp.int32)


def assemble_front(kid_values, kid_rows):
    front_sum = jnp.zeros((VECS, PIV + UPD), jnp.float32)
    front_sum = front_sum.at[:, kid_rows[0]].add(kid_values[0])
    return front_sum.at[:, kid_rows[1]].add(kid_values[1])


def pick_front(front_values, kid_rows):
    return jnp.stack([front_values[:, kid_rows[0]], front_values[:, kid_rows[1]]])


def reference(pivot_rhs, subtree_update, lower_pivot, lower_update, row_map, root_inverse):
    solved_levels = []
    reduced = subtree_update
    for tree_level in range(1, LEVELS + 1):
        spread = 2 ** tree_level
        front_count = N_LEAF // spread
        pivot_factor = lower_pivot[tree_level - 1, ::spread].astype(jnp.float32)
        update_factor = lower_update[tree_level - 1, ::spread].astype(jnp.float32)
        targets = front_targets(row_map[tree_level - 1, ::spread])
        assembled = jax.vmap(assemble_front)(reduced.reshape(front_count, 2, VECS, UPD), targets)
        right_side = front_rhs(pivot_rhs, tree_level) + assembled[:, :, :PIV]
        solution = jnp.einsum("fip,fvp->fvi", pivot_factor, right_side, precision=HIGHEST_PRECISION)
        solved_levels.append(solution)
        reduced = assembled[:, :, PIV:] - jnp.einsum("frp,fvp->fvr", update_factor, solution, precision=HIGHEST_PRECISION)
    root_values = jnp.dot(reduced[0], root_inverse.astype(jnp.float32).T, precision=HIGHEST_PRECISION)
    known = root_values[None]
    pieces = [None] * LEVELS
    for tree_level in range(LEVELS, 0, -1):
        spread = 2 ** tree_level
        front_count = N_LEAF // spread
        pivot_factor = lower_pivot[tree_level - 1, ::spread].astype(jnp.float32)
        update_factor = lower_update[tree_level - 1, ::spread].astype(jnp.float32)
        targets = front_targets(row_map[tree_level - 1, ::spread])
        coupling = jnp.einsum("frp,fvr->fvp", update_factor, known, precision=HIGHEST_PRECISION)
        residual_part = solved_levels[tree_level - 1] - coupling
        solution = jnp.einsum("fip,fvi->fvp", pivot_factor, residual_part, precision=HIGHEST_PRECISION)
        pieces[tree_level - 1] = leaf_layout(solution, tree_level)
        whole_front = jnp.concatenate([solution, known], axis=2)
        known = jax.vmap(pick_front)(whole_front, targets).reshape(2 * front_count, VECS, UPD)
    return jnp.concatenate(pieces, axis=1), known
```

```python
import functools

import jax
import jax.numpy as jnp
from jax import lax
from jax.experimental import pallas as pl
from jax.experimental.pallas import tpu as pltpu
from jax.sharding import PartitionSpec as P

MESH = pl.DeviceIdType.MESH
PANEL_AXIS, LEAF_AXIS = "panel", "leaf"
(CURRENT, SWAPPED, KEPT, RHS, GATHER, SOLVED, PAIR, PART,
 LAND, RELAY, KNOWN, CHILD, OWN, PIVOT_IN, UPDATE_IN, MAPS,
 PIVOT_SOLUTION, SUBTREE_SOLUTION, PIVOTS, UPDATES, ROOT, LOWER_PIVOT, LOAD_SEM, LOWER_UPDATE,
 ROOT_INVERSE, TABLES, ROOT_T, UPDATES_T, PIVOTS_T, TABLES_T, SEND_SEM, RECV_SEM,
 CROSS_SEM, SWAP_SEND_SEM, SWAP_RECV_SEM, TALLY, PIVOT_RHS, SUBTREE_UPDATE, ROW_MAP) = range(39)
OUTER_MAX = 4
TURNS = (8, 4, 4, 4)
DIRECT_PANELS = 8
BATCHES = 2
VMEM_LIMIT = 60 * 2 ** 20
NT = (((1,), (1,)), ((), ()))
NN = (((1,), (0,)), ((), ()))


def bit_reverse(value, bits):
    out = 0
    for i in range(bits):
        out |= (value >> i & 1) << (bits - 1 - i)
    return out


def split(x):
    high = x.astype(jnp.bfloat16).astype(jnp.float32)
    return jnp.concatenate([high, x - high], 0).astype(jnp.bfloat16)


def fold(x):
    half = x.shape[0] // 2
    return x[:half] + x[half:]


def dot(x, w, dims):
    return lax.dot_general(x, w, dims, preferred_element_type=jnp.float32)


def loop(low, high, step, carry):
    if high - low <= 8:
        for i in range(low, high):
            carry = step(i, carry)
        return carry
    return lax.fori_loop(low, high, step, carry)


def kernel(levels, batches, outer, inner, names, *args):
    ref = dict(zip(names, args))
    pivot_in, update_in, maps = ref[PIVOT_IN], ref[UPDATE_IN], ref[MAPS]
    pivot_out, update_out = ref[PIVOT_SOLUTION], ref[SUBTREE_SOLUTION]
    pivots, updates, root = ref[PIVOTS], ref[UPDATES], ref[ROOT]
    panels = outer * inner
    pivot_block, update_block = pivot_in.shape[2], update_in.shape[2]
    whole_vectors = update_in.shape[1]
    vectors = whole_vectors // batches
    slots = pivot_block + update_block
    group = vectors >> levels
    merged = panels <= DIRECT_PANELS

    leaf = lax.axis_index(LEAF_AXIS)
    panel = lax.axis_index(PANEL_AXIS)
    row, col = panel // inner, panel % inner

    bits = [(leaf >> level) & 1 for level in range(levels)]
    counts = [vectors >> (level + 1) for level in range(levels)]
    offsets = [sum(whole_vectors >> (below + 1) for below in range(level)) for level in range(levels)]

    def block_of(index, size):
        return pl.ds(pl.multiple_of(index * size, size), size)

    loads = []
    for level in range(levels):
        loads.append(pltpu.make_async_copy(
            ref[LOWER_PIVOT].at[level, 0], pivots.at[level], ref[LOAD_SEM].at[2 * level]))
        loads.append(pltpu.make_async_copy(
            ref[LOWER_UPDATE].at[level, 0], updates.at[level], ref[LOAD_SEM].at[2 * level + 1]))
    loads.append(pltpu.make_async_copy(ref[ROOT_INVERSE], root, ref[LOAD_SEM].at[2 * levels]))
    fetches = [pltpu.make_async_copy(ref[source], ref[target], ref[LOAD_SEM].at[2 * levels + 1 + i]) for i, (source, target) in enumerate(
        ((ROW_MAP, MAPS), (SUBTREE_UPDATE, UPDATE_IN), (PIVOT_RHS, PIVOT_IN)))]

    barrier = pltpu.get_barrier_semaphore()
    for d in range(1, outer):
        pl.semaphore_signal(barrier, 1, device_id={PANEL_AXIS: (row ^ d) * inner + col}, device_id_type=MESH)
    for e in range(1, inner):
        pl.semaphore_signal(barrier, 1, device_id={PANEL_AXIS: row * inner + (col ^ e)}, device_id_type=MESH)
    if merged:
        for d in range(1, outer):
            for e in range(1, inner):
                pl.semaphore_signal(
                    barrier, 1, device_id={PANEL_AXIS: (row ^ d) * inner + (col ^ e)}, device_id_type=MESH)
    for level in range(1 if merged else levels):
        pl.semaphore_signal(barrier, 1, device_id={LEAF_AXIS: leaf ^ (1 << level)}, device_id_type=MESH)
    if merged:
        for level in range(1, levels):
            for d in range(outer):
                for e in range(inner):
                    pl.semaphore_signal(
                        barrier, 1, device_id={LEAF_AXIS: leaf ^ (1 << level), PANEL_AXIS: (row ^ d) * inner + (col ^ e)},
                        device_id_type=MESH)

    for copy in fetches:
        copy.start()
    loads[0].start()
    fetches[0].wait()
    tables = ref[TABLES]
    chunk = min(128, slots)

    def build(level):
        for side in range(2):
            child = bits[level] if side == 0 else 1 - bits[level]
            target = maps[level, 0, pl.ds(child, 1), :]

            def fill(i, _):
                rows = lax.broadcasted_iota(jnp.int32, (chunk, update_block), 0) + i * chunk
                tables[level, side, block_of(i, chunk), :] = jnp.where(rows == target, 1.0, 0.0).astype(jnp.bfloat16)
                return _
            lax.fori_loop(0, slots // chunk, fill, 0)
            if merged:
                ref[TABLES_T][level, side] = tables[level, side].T

    build(0)

    for copy in loads[1:]:
        copy.start()
    for copy in fetches[1:]:
        copy.wait()
    for batch in range(batches):
        first = ref[CURRENT, 0, batch]
        for g in range(1 << levels):
            for k in range(group):
                first[pl.ds(g * group + k, 1), :] = update_in[0, pl.ds(batch * vectors + (k << levels | bit_reverse(g, levels)), 1), :]
        for level in range(levels):
            size = levels - 1 - level
            for g in range(1 << size):
                for k in range(group):
                    ref[RHS, level, batch][pl.ds(g * group + k, 1), :] = pivot_in[
                        0, pl.ds(offsets[level] + batch * counts[level] + (k << size | bit_reverse(g, size)), 1), :]

    loaded = set()
    turned = {}
    pieces = 4

    def load(index):
        if index not in loaded:
            loaded.add(index)
            loads[index].wait()

    def turn(index):
        load(index)
        at_piece = turned.get(index, 0)
        turned[index] = at_piece + 1
        level, odd = index // 2, index % 2
        for j in range(at_piece * panels // pieces, (at_piece + 1) * panels // pieces):
            if index == 2 * levels:
                part = slice(j * update_block, (j + 1) * update_block)
                ref[ROOT_T][part, :] = root[:, part].T
            elif odd:
                part = slice(j * update_block, (j + 1) * update_block)
                ref[UPDATES_T][level, :, part] = updates[level, part, :].T
            else:
                part = slice(j * pivot_block, (j + 1) * pivot_block)
                ref[PIVOTS_T][level, part, :] = pivots[level, :, part].T

    def turn_some(count):
        for index in range(2 * levels + 1):
            while count and turned.get(index, 0) < pieces:
                turn(index)
                count -= 1

    def ready(index):
        load(index)
        while merged and turned.get(index, 0) < pieces:
            turn(index)

    if merged:
        pl.semaphore_wait(barrier, panels - 1 + 1 + (levels - 1) * panels)
    else:
        pl.semaphore_wait(barrier, outer - 1 + inner - 1 + levels)

    row_order = [d for d in (1, 3, 2) if d < outer]
    far_order = [d for d in (3, 2, 1) if d < outer]

    def place(d, e):
        return (row ^ d) * inner + (col ^ e)

    def send(source, target, which, slot, device):
        batch, which = which
        return pltpu.make_async_remote_copy(
            src_ref=source, dst_ref=target, send_sem=ref[SEND_SEM].at[batch, which, slot],
            recv_sem=ref[RECV_SEM].at[batch, which, slot], device_id=device, device_id_type=MESH)

    def to_row(source, target, which, slot, d):
        return send(source, target, which, slot, {PANEL_AXIS: (row ^ d) * inner + col})

    def to_col(source, target, which, slot, e):
        return send(source, target, which, slot, {PANEL_AXIS: row * inner + (col ^ e)})

    half_panels = panels // 2
    near = range(1, half_panels)
    distant = range(half_panels, panels)
    order = list(range(2 * levels + 1))
    for level in range(levels - 1, -1, -1):
        order += [2 * levels + 1 + 2 * level, 2 * levels + 2 + 2 * level]
    sent = {}

    def arrival(which, kind, slot):
        batch, which = which
        group = 0 if slot < half_panels else 1 + slot - half_panels
        if kind == 1:
            level = (which - 1) // 2 if which < 2 * levels else levels - 1 + (which - 2 * levels - 1) // 2
            return ref[CROSS_SEM].at[batch, level, group]
        return ref[RECV_SEM].at[batch, order.index(which) % 2, 1 + half_panels if kind == 2 else group]

    def hand(source, target, which, kind, slot, device):
        return pltpu.make_async_remote_copy(
            src_ref=source, dst_ref=target, send_sem=ref[SEND_SEM].at[which[0], which[1]],
            recv_sem=arrival(which, kind, slot), device_id=device, device_id_type=MESH)

    def ship(source, target, which, kind, slot, hop, panel_to):
        device = {PANEL_AXIS: panel_to}
        if hop:
            device[LEAF_AXIS] = leaf ^ hop
        hand(source, target, which, kind, slot, device).start()
        sent[which] = sent.get(which, 0) + source.shape[0] * source.shape[1] // update_block

    def landed(target, which, kind, slot):
        hand(target, target, which, kind, slot, {PANEL_AXIS: panel ^ 1}).wait_recv()

    def at(slot):
        return place(slot // inner, slot % inner)

    def gather_direct(which, buf, value, use, acc, halved, hop=0, other=None, bit=None):
        rows = pl.ds(0, buf.shape[1])
        other_rows = rows
        if hop:
            half = buf.shape[1] // 2
            rows, other_rows = block_of(bit, half), block_of(1 - bit, half)
        if value is not None:
            buf[0] = value
        far = [half_panels] if halved else list(distant)[::-1]
        for slot in far + list(near)[::-1] + ([0] if hop else []):
            if hop:
                ship(other, buf.at[slot, rows], which, 1, slot, hop, at(slot))
            if slot:
                ship(buf.at[0, rows], buf.at[slot, rows], which, 0, slot, 0, at(slot))
        yield

        def take(slots, other_slots, slot):
            landed(buf.at[slots, rows], which, 0, slot)
            if hop:
                landed(buf.at[other_slots, other_rows], which, 1, slot)

        if halved:
            take(half_panels, half_panels, half_panels)
            for slot in near:
                ship(buf.at[half_panels], buf.at[half_panels + slot], which, 0, half_panels + slot, 0, at(slot))
            acc = use(acc, buf[half_panels], at(half_panels))
        if not hop and not halved:
            acc = use(acc, buf[0], at(0))
        take(pl.ds(1, half_panels - 1), pl.ds(0, half_panels), 0)
        for slot in ([0] if hop or halved else []) + list(near):
            acc = use(acc, buf[slot], at(slot))
        if halved:
            yield
        for slot in list(distant)[halved:]:
            landed(buf.at[slot], which, 0, slot)
            acc = use(acc, buf[slot], at(slot))
        return acc

    def scatter_direct(which, part_buf, in_buf, part, halved, relay_buf=None, hop=0, bit=None, base=None):
        count = part_buf.shape[1]
        half = count // 2 if hop else count
        rows = block_of(bit, half) if hop else pl.ds(0, half)
        other_rows = block_of(1 - bit, half) if hop else rows

        def go(slot):
            if hop:
                ship(part_buf.at[slot, other_rows], in_buf.at[1, slot], which, 1, slot, hop, at(slot))
            if slot:
                ship(part_buf.at[slot, rows], in_buf.at[0, slot], which, 0, slot, 0, at(slot))

        def fill(slot):
            part_buf[slot] = part(at(slot))

        if halved:
            for slot in list(near)[::-1]:
                fill(half_panels + slot)
                ship(part_buf.at[half_panels + slot], relay_buf.at[slot], which, 2, slot, 0, at(slot))
            fill(half_panels)
            first = list(near)[::-1]
        else:
            first = list(distant)[::-1] + list(near)[::-1]
        for slot in first:
            fill(slot)
            go(slot)
        own = part(at(0))
        if hop:
            part_buf[0] = base[...] - own
            go(0)
        else:
            own = own if base is None else base[...] - own
        yield
        if halved:
            total = part_buf[half_panels]
            landed(relay_buf.at[pl.ds(1, half_panels - 1)], which, 2, 0)
            for slot in near:
                total = total + relay_buf[slot]
            part_buf[half_panels] = total
            go(half_panels)
            yield
        sources = [half_panels] if halved else list(distant)
        sign = 1 if base is None else -1
        acc = part_buf[0, rows, :] if hop else own
        landed(in_buf.at[0, pl.ds(1, half_panels - 1)], which, 0, 0)
        for slot in near:
            acc = acc + sign * in_buf[0, slot]
        for slot in sources:
            landed(in_buf.at[0, slot], which, 0, slot)
            acc = acc + sign * in_buf[0, slot]
        if not hop:
            return acc
        landed(in_buf.at[1, pl.ds(0, half_panels)], which, 1, 0)
        there = in_buf[1, 0]
        for slot in near:
            there = there - in_buf[1, slot]
        for slot in sources:
            landed(in_buf.at[1, slot], which, 1, slot)
            there = there - in_buf[1, slot]
        return acc, there

    def gather(which, buf, value, use, acc):
        buf[0] = value
        for d in far_order:
            to_row(buf.at[0], buf.at[d * inner], which, d * inner, d).start()

        def forward(d):
            def go(e, _):
                to_col(buf.at[d * inner], buf.at[d * inner + e], which, d * inner + e, e).start()
                return _
            loop(1, inner, go, 0)

        def arrived(d, acc):
            def go(e, acc):
                slot = d * inner + e
                to_col(buf.at[slot], buf.at[slot], which, slot, e).wait_recv()
                return use(acc, buf[slot], place(d, e))
            return loop(1, inner, go, acc)

        forward(0)
        acc = use(acc, buf[0], place(0, 0))
        yield
        last = 0
        for d in row_order:
            to_row(buf.at[d * inner], buf.at[d * inner], which, d * inner, d).wait_recv()
            forward(d)
            acc = use(acc, buf[d * inner], place(d, 0))
            acc = arrived(last, acc)
            last = d
        yield
        return arrived(last, acc)

    def scatter(which, part_buf, in_buf, part):
        for d in far_order + [0]:
            def go(e, _, d=d):
                slot = d * inner + e
                part_buf[slot] = part(place(d, e))
                to_col(part_buf.at[slot], in_buf.at[slot], which, slot, e).start()
                return _
            loop(1, inner, go, 0)

        yield

        def collect(d):
            def go(e, acc):
                slot = d * inner + e
                to_col(in_buf.at[slot], in_buf.at[slot], which, slot, e).wait_recv()
                return acc + in_buf[slot]
            return loop(1, inner, go, part(place(d, 0)))

        for d in far_order:
            slot = d * inner
            part_buf[slot] = collect(d)
            to_row(part_buf.at[slot], in_buf.at[slot], which, slot, d).start()
        acc = collect(0)
        yield
        for d in row_order:
            slot = d * inner
            to_row(in_buf.at[slot], in_buf.at[slot], which, slot, d).wait_recv()
            acc = acc + in_buf[slot]
        return acc

    def swap(source, target, which, level):
        return pltpu.make_async_remote_copy(
            src_ref=source, dst_ref=target, send_sem=ref[SWAP_SEND_SEM].at[which[0], which[1]],
            recv_sem=ref[SWAP_RECV_SEM].at[which[0], which[1]], device_id={LEAF_AXIS: leaf ^ (1 << level)},
            device_id_type=MESH)

    swaps = []

    def begin_swap(level, batch):
        count = counts[level]
        copy = swap(ref[CURRENT, level, batch].at[block_of(1 - bits[level], count)],
                    ref[SWAPPED, level, batch], (batch, level), level)
        copy.start()
        swaps.append(copy)
        return copy

    def spread(level, side, value):
        if merged:
            return dot(split(value), ref[TABLES_T][level, side], NN)
        return dot(split(value), tables[level, side], NT)

    def run(batch):
        vertical = None
        for level in range(levels):
            count = counts[level]
            top = level == 0
            current = ref[CURRENT, level, batch]
            if merged and not top:
                mine, other = vertical
                total = spread(level, 0, mine) + spread(level, 1, other)
            else:
                copy = begin_swap(level, batch)
                yield
                total = spread(level, 0, current[block_of(bits[level], count), :])
                copy.wait_recv()
                total = total + spread(level, 1, ref[SWAPPED, level, batch][...])
            assembled = fold(total)
            kept = ref[KEPT, level, batch]
            kept[...] = assembled[:, pivot_block:]
            if not merged:
                ready(2 * level)

            def use(acc, value, index, level=level):
                ready(2 * level)
                if merged:
                    return acc + dot(split(value), ref[PIVOTS_T][level, block_of(index, pivot_block), :], NN)
                return acc + dot(split(value), pivots[level, :, block_of(index, pivot_block)], NT)

            which = 2 * level
            value = ref[RHS, level, batch][...] + assembled[:, :pivot_block]
            zero = jnp.zeros((2 * count, pivot_block), jnp.float32)
            if merged:
                solved = yield from gather_direct(
                    (batch, which), ref[GATHER, which, batch], value, use, zero, level < levels - 1)
            else:
                solved = yield from gather((batch, which), ref[GATHER, which, batch], value, use, zero)
            solved = fold(solved)
            ref[SOLVED, level, batch][...] = solved
            pair = ref[PAIR, level, batch]
            pair[...] = split(solved)
            ready(2 * level + 1)

            def part(index, level=level, pair=pair):
                if merged:
                    return fold(dot(pair[...], ref[UPDATES_T][level, :, block_of(index, update_block)], NN))
                return fold(dot(pair[...], updates[level, block_of(index, update_block), :], NT))

            which = 2 * level + 1
            buffers = ref[PART, which, batch], ref[LAND, which, batch]
            last = level == levels - 1
            if not merged:
                coupled = yield from scatter((batch, which), *buffers, part)
                ref[CURRENT, level + 1, batch][...] = kept[...] - coupled
            elif last:
                vertical = yield from scatter_direct((batch, which), *buffers, part, level < levels - 1, ref[RELAY, which, batch], base=kept)
            else:
                vertical = yield from scatter_direct(
                    (batch, which), *buffers, part, level < levels - 1, ref[RELAY, which, batch],
                    1 << (level + 1), bits[level + 1], kept)

        if not merged:
            ready(2 * levels)
        count = counts[levels - 1]

        def use_root(acc, value, index):
            ready(2 * levels)
            if merged:
                return acc + dot(split(value), ref[ROOT_T][block_of(index, update_block), :], NN)
            return acc + dot(split(value), root[:, block_of(index, update_block)], NT)

        zero = jnp.zeros((2 * count, update_block), jnp.float32)
        buf = ref[GATHER, 2 * levels, batch]
        if merged:
            known = yield from gather_direct((batch, 2 * levels), buf, vertical, use_root, zero, False)
        else:
            known = yield from gather((batch, 2 * levels), buf, ref[CURRENT, levels, batch][...], use_root, zero)
        ref[KNOWN, levels, batch][...] = fold(known)

        for level in range(levels - 1, -1, -1):
            count = counts[level]
            top = level == 0
            last = level == levels - 1
            which = 2 * levels + 1 + 2 * level

            def use(acc, value, index, level=level):
                return acc + dot(split(value), updates[level, block_of(index, update_block), :], NN)

            zero = jnp.zeros((2 * count, pivot_block), jnp.float32)
            buf = ref[GATHER, which, batch]
            if not merged:
                known = ref[KNOWN, level + 1, batch]
                coupling = yield from gather((batch, which), buf, known[...], use, zero)
            elif last:
                coupling = yield from gather_direct(
                    (batch, which), buf, ref[KNOWN, levels, batch][...], use, zero, level < levels - 1)
            else:
                coupling = yield from gather_direct(
                    (batch, which), buf, None, use, zero, level < levels - 1, 1 << (level + 1),
                    ref[CHILD, level + 1, batch], bits[level + 1])
            coupling = fold(coupling)
            pair = ref[PAIR, level, batch]
            pair[...] = split(ref[SOLVED, level, batch][...] - coupling)

            def part(index, level=level, pair=pair):
                return fold(dot(pair[...], pivots[level, :, block_of(index, pivot_block)], NN))

            which = which + 1
            buffers = ref[PART, which, batch], ref[LAND, which, batch]
            if merged:
                own = yield from scatter_direct(
                    (batch, which), *buffers, part, level < levels - 1, ref[RELAY, which, batch])
                known = ref[GATHER, which - 1, batch][0]
            else:
                own = yield from scatter((batch, which), *buffers, part)
                known = ref[KNOWN, level + 1, batch][...]
            own_pair, known_pair = split(own), split(known)

            def child(side):
                return fold(dot(own_pair, tables[level, side, :pivot_block, :], NN)
                            + dot(known_pair, tables[level, side, pivot_block:, :], NN))

            ref[CHILD, level, batch][...] = child(1)
            rows = block_of(bits[level], count)
            exchange = top or not merged
            if exchange:
                copy = swap(ref[CHILD, level, batch], ref[KNOWN, level, batch].at[rows], (batch, 1 if merged else levels + level), level)
                copy.start()
                swaps.append(copy)
                ref[KNOWN, level, batch][rows, :] = child(0)
            else:
                ref[GATHER, 2 * levels + 1 + 2 * (level - 1), batch][0, rows, :] = child(0)
            ref[OWN, level, batch][...] = own
            size = levels - 1 - level

            def emit(level=level, count=count, size=size):
                for g in range(1 << size):
                    for k in range(group):
                        pivot_out[0, pl.ds(offsets[level] + batch * count + (k << size | bit_reverse(g, size)), 1), :] = (
                            ref[OWN, level, batch][pl.ds(g * group + k, 1), :])
            emits.append(emit)
            if exchange:
                emit_all()
                yield
                copy.wait_recv()

        known = ref[KNOWN, 0, batch]
        for g in range(1 << levels):
            for k in range(group):
                update_out[0, pl.ds(batch * vectors + (k << levels | bit_reverse(g, levels)), 1), :] = known[pl.ds(g * group + k, 1), :]

    emits = []

    def emit_all():
        while emits:
            emits.pop()()

    runs = [run(batch) for batch in range(batches)]
    for one in runs:
        next(one)
    for level in range(1, levels):
        build(level)
    turns = list(TURNS)
    while runs:
        runs = [one for one in runs if next(one, True) is None]
        if merged and turns:
            turn_some(turns.pop(0))

    for copy in swaps:
        copy.wait_send()
    tally = ref[TALLY]
    for which, count in sent.items():
        hand(tally.at[pl.ds(0, count)], tally.at[pl.ds(0, count)], which, 0, 1, {PANEL_AXIS: panel ^ 1}).wait_send()
    for which in range(0 if merged else 4 * levels + 1):
        for batch in range(batches):
            name = (GATHER, which, batch)
            buf = ref[name] if name in ref else ref[PART, which, batch]

            def finish(slot, _, which=which, batch=batch, buf=buf):
                send(buf.at[slot], buf.at[slot], (batch, which), slot, {PANEL_AXIS: panel ^ 1}).wait_send()
                return _
            lax.fori_loop(1, panels, finish, 0)


def hand_over(pivot_in, update_in, pivot_out, update_out):
    update_out[...] = update_in[...]
    pivot_out[...] = pivot_in[...]


def local(panels, pivot_rhs, subtree_update, lower_pivot, lower_update, row_map, root_inverse):
    levels = lower_pivot.shape[0]
    pivot_block, update_block = pivot_rhs.shape[2], subtree_update.shape[2]
    batches = BATCHES if subtree_update.shape[1] >> levels >= 8 * BATCHES else 1
    vectors = subtree_update.shape[1] // batches
    outer = min(OUTER_MAX, panels)
    inner = panels // outer
    slots = pivot_block + update_block
    merged = panels <= DIRECT_PANELS
    whole_rows = vectors // 2
    f32, bf16 = jnp.float32, jnp.bfloat16
    scratch = {
        PIVOTS: pltpu.VMEM((levels,) + lower_pivot.shape[2:], bf16),
        UPDATES: pltpu.VMEM((levels,) + lower_update.shape[2:], bf16),
        ROOT: pltpu.VMEM(root_inverse.shape, bf16),
        TABLES: pltpu.VMEM((levels, 2, slots, update_block), bf16),
    }
    if merged:
        scratch[TABLES_T] = pltpu.VMEM((levels, 2, update_block, slots), bf16)
        scratch[PIVOTS_T] = pltpu.VMEM((levels, lower_pivot.shape[3], pivot_block), bf16)
        scratch[UPDATES_T] = pltpu.VMEM((levels, pivot_block, lower_update.shape[2]), bf16)
        scratch[ROOT_T] = pltpu.VMEM((root_inverse.shape[1], update_block), bf16)
    for batch in range(batches):
        for level in range(levels):
            count = vectors >> (level + 1)
            back = 2 * levels + 1 + 2 * level
            scratch[CURRENT, level, batch] = pltpu.VMEM((2 * count, update_block), f32)
            scratch[KNOWN, level, batch] = pltpu.VMEM((2 * count, update_block), f32)
            scratch[SWAPPED, level, batch] = pltpu.VMEM((count, update_block), f32)
            scratch[CHILD, level, batch] = pltpu.VMEM((count, update_block), f32)
            scratch[KEPT, level, batch] = pltpu.VMEM((count, update_block), f32)
            scratch[SOLVED, level, batch] = pltpu.VMEM((count, pivot_block), f32)
            scratch[RHS, level, batch] = pltpu.VMEM((count, pivot_block), f32)
            scratch[OWN, level, batch] = pltpu.VMEM((count, pivot_block), f32)
            scratch[PAIR, level, batch] = pltpu.VMEM((2 * count, pivot_block), bf16)
            scratch[GATHER, 2 * level, batch] = pltpu.VMEM((panels, count, pivot_block), f32)
            scratch[GATHER, back, batch] = pltpu.VMEM((panels, count, update_block), f32)
            for which, width in ((2 * level + 1, update_block), (back + 1, pivot_block)):
                scratch[PART, which, batch] = pltpu.VMEM((panels, count, width), f32)
                if not merged:
                    scratch[LAND, which, batch] = pltpu.VMEM((panels, count, width), f32)
                elif which == 2 * level + 1 and level < levels - 1:
                    scratch[LAND, which, batch] = pltpu.VMEM((2, panels, count // 2, width), f32)
                else:
                    scratch[LAND, which, batch] = pltpu.VMEM((1, panels, count, width), f32)
                if merged:
                    scratch[RELAY, which, batch] = pltpu.VMEM((panels // 2, count, width), f32)
        count = vectors >> levels
        scratch[CURRENT, levels, batch] = pltpu.VMEM((count, update_block), f32)
        scratch[KNOWN, levels, batch] = pltpu.VMEM((count, update_block), f32)
        scratch[GATHER, 2 * levels, batch] = pltpu.VMEM((panels, count, update_block), f32)
    if merged:
        scratch[SEND_SEM] = pltpu.SemaphoreType.DMA((batches, 4 * levels + 1))
        scratch[RECV_SEM] = pltpu.SemaphoreType.DMA((batches, 2, 2 + panels // 2))
        scratch[CROSS_SEM] = pltpu.SemaphoreType.DMA((batches, max(1, 2 * levels - 2), 2))
    else:
        scratch[SEND_SEM] = pltpu.SemaphoreType.DMA((batches, 4 * levels + 1, panels))
        scratch[RECV_SEM] = pltpu.SemaphoreType.DMA((batches, 4 * levels + 1, panels))
    scratch[MAPS] = pltpu.VMEM(row_map.shape, jnp.int32)
    scratch[UPDATE_IN] = pltpu.VMEM(subtree_update.shape, f32)
    scratch[PIVOT_IN] = pltpu.VMEM(pivot_rhs.shape, f32)
    scratch[TALLY] = pltpu.VMEM((panels * whole_rows if merged else 8, update_block), f32)
    scratch[SWAP_SEND_SEM] = pltpu.SemaphoreType.DMA((batches, 2 if merged else 2 * levels))
    scratch[SWAP_RECV_SEM] = pltpu.SemaphoreType.DMA((batches, 2 if merged else 2 * levels))
    scratch[LOAD_SEM] = pltpu.SemaphoreType.DMA((2 * levels + 4,))
    names = [PIVOT_RHS, SUBTREE_UPDATE, ROW_MAP, LOWER_PIVOT, LOWER_UPDATE, ROOT_INVERSE,
             PIVOT_SOLUTION, SUBTREE_SOLUTION] + list(scratch)
    vmem, anywhere = pl.BlockSpec(memory_space=pltpu.VMEM), pl.BlockSpec(memory_space=pl.ANY)
    results = pl.pallas_call(
        functools.partial(kernel, levels, batches, outer, inner, names),
        out_shape=(jax.ShapeDtypeStruct(pivot_rhs.shape, f32),
                   jax.ShapeDtypeStruct(subtree_update.shape, f32)),
        in_specs=[anywhere] * 6,
        out_specs=(vmem, vmem),
        scratch_shapes=list(scratch.values()),
        compiler_params=pltpu.CompilerParams(collective_id=0, has_side_effects=True, vmem_limit_bytes=VMEM_LIMIT),
    )(pivot_rhs, subtree_update, row_map, lower_pivot, lower_update, root_inverse)
    return pl.pallas_call(
        hand_over,
        out_shape=tuple(jax.ShapeDtypeStruct(one.shape, f32) for one in results),
        in_specs=[vmem] * 2,
        out_specs=(vmem, vmem),
    )(*results)


def solution(mesh):
    in_specs = (
        P(LEAF_AXIS, None, PANEL_AXIS),
        P(LEAF_AXIS, None, PANEL_AXIS),
        P(None, LEAF_AXIS, PANEL_AXIS, None),
        P(None, LEAF_AXIS, None, PANEL_AXIS),
        P(None, LEAF_AXIS, None, PANEL_AXIS),
        P(PANEL_AXIS, None),
    )
    out_specs = (P(LEAF_AXIS, None, PANEL_AXIS), P(LEAF_AXIS, None, PANEL_AXIS))
    return jax.shard_map(functools.partial(local, mesh.shape[PANEL_AXIS]), mesh=mesh, in_specs=in_specs,
                         out_specs=out_specs, check_vma=False)
```

```python
import functools

import jax
import jax.numpy as jnp
from jax import lax
from jax.experimental import pallas as pl
from jax.experimental.pallas import tpu as pltpu
from jax.sharding import PartitionSpec as P

MESH = pl.DeviceIdType.MESH
PANEL_AXIS, LEAF_AXIS = "panel", "leaf"
(CURRENT, SWAPPED, KEPT, RHS, GATHER, SOLVED, PAIR, PART,
 LAND, RELAY, KNOWN, CHILD, OWN, PIVOT_IN, UPDATE_IN, MAPS,
 PIVOT_SOLUTION, SUBTREE_SOLUTION, PIVOTS, UPDATES, ROOT, LOWER_PIVOT, LOAD_SEM, LOWER_UPDATE,
 ROOT_INVERSE, TABLES, ROOT_T, UPDATES_T, PIVOTS_T, TABLES_T, SEND_SEM, RECV_SEM,
 CROSS_SEM, SWAP_SEND_SEM, SWAP_RECV_SEM, TALLY, PIVOT_RHS, SUBTREE_UPDATE, ROW_MAP) = range(39)
OUTER_MAX = 4
TURNS = (8, 4, 4, 4)
DIRECT_PANELS = 8
FAR_ORDER = (3, 1, 2, 0)
BATCHES = 2
VMEM_LIMIT = 60 * 2 ** 20
NT = (((1,), (1,)), ((), ()))
NN = (((1,), (0,)), ((), ()))


def bit_reverse(value, bits):
    out = 0
    for i in range(bits):
        out |= (value >> i & 1) << (bits - 1 - i)
    return out


def split(x):
    high = x.astype(jnp.bfloat16).astype(jnp.float32)
    return jnp.concatenate([high, x - high], 0).astype(jnp.bfloat16)


def fold(x):
    half = x.shape[0] // 2
    return x[:half] + x[half:]


def dot(x, w, dims):
    return lax.dot_general(x, w, dims, preferred_element_type=jnp.float32)


def loop(low, high, step, carry):
    if high - low <= 8:
        for i in range(low, high):
            carry = step(i, carry)
        return carry
    return lax.fori_loop(low, high, step, carry)


def kernel(levels, batches, outer, inner, names, *args):
    ref = dict(zip(names, args))
    pivot_in, update_in, maps = ref[PIVOT_IN], ref[UPDATE_IN], ref[MAPS]
    pivot_out, update_out = ref[PIVOT_SOLUTION], ref[SUBTREE_SOLUTION]
    pivots, updates, root = ref[PIVOTS], ref[UPDATES], ref[ROOT]
    panels = outer * inner
    pivot_block, update_block = pivot_in.shape[2], update_in.shape[2]
    whole_vectors = update_in.shape[1]
    vectors = whole_vectors // batches
    slots = pivot_block + update_block
    group = vectors >> levels
    merged = panels <= DIRECT_PANELS

    leaf = lax.axis_index(LEAF_AXIS)
    panel = lax.axis_index(PANEL_AXIS)
    row, col = panel // inner, panel % inner

    bits = [(leaf >> level) & 1 for level in range(levels)]
    counts = [vectors >> (level + 1) for level in range(levels)]
    offsets = [sum(whole_vectors >> (below + 1) for below in range(level)) for level in range(levels)]

    def block_of(index, size):
        return pl.ds(pl.multiple_of(index * size, size), size)

    loads = []
    for level in range(levels):
        loads.append(pltpu.make_async_copy(
            ref[LOWER_PIVOT].at[level, 0], pivots.at[level], ref[LOAD_SEM].at[2 * level]))
        loads.append(pltpu.make_async_copy(
            ref[LOWER_UPDATE].at[level, 0], updates.at[level], ref[LOAD_SEM].at[2 * level + 1]))
    loads.append(pltpu.make_async_copy(ref[ROOT_INVERSE], root, ref[LOAD_SEM].at[2 * levels]))
    fetches = [pltpu.make_async_copy(ref[source], ref[target], ref[LOAD_SEM].at[2 * levels + 1 + i]) for i, (source, target) in enumerate(
        ((ROW_MAP, MAPS), (SUBTREE_UPDATE, UPDATE_IN), (PIVOT_RHS, PIVOT_IN)))]

    barrier = pltpu.get_barrier_semaphore()
    for d in range(1, outer):
        pl.semaphore_signal(barrier, 1, device_id={PANEL_AXIS: (row ^ d) * inner + col}, device_id_type=MESH)
    for e in range(1, inner):
        pl.semaphore_signal(barrier, 1, device_id={PANEL_AXIS: row * inner + (col ^ e)}, device_id_type=MESH)
    if merged:
        for d in range(1, outer):
            for e in range(1, inner):
                pl.semaphore_signal(
                    barrier, 1, device_id={PANEL_AXIS: (row ^ d) * inner + (col ^ e)}, device_id_type=MESH)
    for level in range(1 if merged else levels):
        pl.semaphore_signal(barrier, 1, device_id={LEAF_AXIS: leaf ^ (1 << level)}, device_id_type=MESH)
    if merged:
        for level in range(1, levels):
            for d in range(outer):
                for e in range(inner):
                    pl.semaphore_signal(
                        barrier, 1, device_id={LEAF_AXIS: leaf ^ (1 << level), PANEL_AXIS: (row ^ d) * inner + (col ^ e)},
                        device_id_type=MESH)

    for copy in fetches:
        copy.start()
    loads[0].start()
    fetches[0].wait()
    tables = ref[TABLES]
    chunk = min(128, slots)

    def build(level):
        for side in range(2):
            child = bits[level] if side == 0 else 1 - bits[level]
            target = maps[level, 0, pl.ds(child, 1), :]

            def fill(i, _):
                rows = lax.broadcasted_iota(jnp.int32, (chunk, update_block), 0) + i * chunk
                tables[level, side, block_of(i, chunk), :] = jnp.where(rows == target, 1.0, 0.0).astype(jnp.bfloat16)
                return _
            lax.fori_loop(0, slots // chunk, fill, 0)
            if merged:
                ref[TABLES_T][level, side] = tables[level, side].T

    build(0)

    for copy in loads[1:]:
        copy.start()
    for copy in fetches[1:]:
        copy.wait()
    for batch in range(batches):
        first = ref[CURRENT, 0, batch]
        for g in range(1 << levels):
            for k in range(group):
                first[pl.ds(g * group + k, 1), :] = update_in[0, pl.ds(batch * vectors + (k << levels | bit_reverse(g, levels)), 1), :]
        for level in range(levels):
            size = levels - 1 - level
            for g in range(1 << size):
                for k in range(group):
                    ref[RHS, level, batch][pl.ds(g * group + k, 1), :] = pivot_in[
                        0, pl.ds(offsets[level] + batch * counts[level] + (k << size | bit_reverse(g, size)), 1), :]

    loaded = set()
    turned = {}
    pieces = 4

    def load(index):
        if index not in loaded:
            loaded.add(index)
            loads[index].wait()

    def turn(index):
        load(index)
        at_piece = turned.get(index, 0)
        turned[index] = at_piece + 1
        level, odd = index // 2, index % 2
        for j in range(at_piece * panels // pieces, (at_piece + 1) * panels // pieces):
            if index == 2 * levels:
                part = slice(j * update_block, (j + 1) * update_block)
                ref[ROOT_T][part, :] = root[:, part].T
            elif odd:
                part = slice(j * update_block, (j + 1) * update_block)
                ref[UPDATES_T][level, :, part] = updates[level, part, :].T
            else:
                part = slice(j * pivot_block, (j + 1) * pivot_block)
                ref[PIVOTS_T][level, part, :] = pivots[level, :, part].T

    def turn_some(count):
        for index in range(2 * levels + 1):
            while count and turned.get(index, 0) < pieces:
                turn(index)
                count -= 1

    def ready(index):
        load(index)
        while merged and turned.get(index, 0) < pieces:
            turn(index)

    if merged:
        pl.semaphore_wait(barrier, panels - 1 + 1 + (levels - 1) * panels)
    else:
        pl.semaphore_wait(barrier, outer - 1 + inner - 1 + levels)

    row_order = [d for d in (1, 3, 2) if d < outer]
    far_order = [d for d in (3, 2, 1) if d < outer]

    def place(d, e):
        return (row ^ d) * inner + (col ^ e)

    def send(source, target, which, slot, device):
        batch, which = which
        return pltpu.make_async_remote_copy(
            src_ref=source, dst_ref=target, send_sem=ref[SEND_SEM].at[batch, which, slot],
            recv_sem=ref[RECV_SEM].at[batch, which, slot], device_id=device, device_id_type=MESH)

    def to_row(source, target, which, slot, d):
        return send(source, target, which, slot, {PANEL_AXIS: (row ^ d) * inner + col})

    def to_col(source, target, which, slot, e):
        return send(source, target, which, slot, {PANEL_AXIS: row * inner + (col ^ e)})

    half_panels = panels // 2
    near = range(1, half_panels)
    distant = range(half_panels, panels)
    order = list(range(2 * levels + 1))
    for level in range(levels - 1, -1, -1):
        order += [2 * levels + 1 + 2 * level, 2 * levels + 2 + 2 * level]
    sent = {}

    def arrival(which, kind, slot):
        batch, which = which
        group = 0 if isinstance(slot, int) and slot < half_panels else 1 + slot - half_panels
        if kind == 1:
            level = (which - 1) // 2 if which < 2 * levels else levels - 1 + (which - 2 * levels - 1) // 2
            return ref[CROSS_SEM].at[batch, level, group]
        return ref[RECV_SEM].at[batch, order.index(which) % 2, 1 + half_panels if kind == 2 else group]

    def hand(source, target, which, kind, slot, device):
        return pltpu.make_async_remote_copy(
            src_ref=source, dst_ref=target, send_sem=ref[SEND_SEM].at[which[0], which[1]],
            recv_sem=arrival(which, kind, slot), device_id=device, device_id_type=MESH)

    def ship(source, target, which, kind, slot, hop, panel_to, times=1):
        device = {PANEL_AXIS: panel_to}
        if hop:
            device[LEAF_AXIS] = leaf ^ hop
        hand(source, target, which, kind, slot, device).start()
        sent[which] = sent.get(which, 0) + times * (source.shape[0] * source.shape[1] // update_block)

    def landed(target, which, kind, slot):
        hand(target, target, which, kind, slot, {PANEL_AXIS: panel ^ 1}).wait_recv()

    def at(slot):
        return place(slot // inner, slot % inner)

    def walk(slots, step, carry):
        for slot in slots:
            carry = step(slot, slot, 1, carry)
        return carry

    def gather_direct(which, buf, value, use, acc, halved, hop=0, other=None, bit=None, prepare=None):
        rows = pl.ds(0, buf.shape[1])
        other_rows = rows
        if hop:
            half = buf.shape[1] // 2
            rows, other_rows = block_of(bit, half), block_of(1 - bit, half)
        if value is not None:
            buf[0] = value
        far = [half_panels] if halved else [half_panels ^ i for i in FAR_ORDER if i < half_panels]
        for slot in far + list(near)[::-1] + ([0] if hop else []):
            if hop:
                ship(other, buf.at[slot, rows], which, 1, slot, hop, at(slot))
            if slot:
                ship(buf.at[0, rows], buf.at[slot, rows], which, 0, slot, 0, at(slot))
        yield
        if prepare is not None and not halved:
            prepare()

        def take(slots, other_slots, slot):
            landed(buf.at[slots, rows], which, 0, slot)
            if hop:
                landed(buf.at[other_slots, other_rows], which, 1, slot)

        def add(slot, _, times, acc):
            return use(acc, buf[slot], at(slot))

        def take_and_add(slot, _, times, acc):
            landed(buf.at[slot], which, 0, slot)
            return use(acc, buf[slot], at(slot))

        if halved:
            take(half_panels, half_panels, half_panels)
            for slot in near:
                ship(buf.at[half_panels], buf.at[half_panels + slot], which, 0, half_panels + slot, 0, at(slot))
            take(pl.ds(1, half_panels - 1), pl.ds(0, half_panels), 0)
            if prepare is not None:
                prepare()
            acc = walk(range(half_panels + 1), add, acc)
            yield
        else:
            take(pl.ds(1, half_panels - 1), pl.ds(0, half_panels), 0)
            acc = walk(range(half_panels), add, acc)
        return walk(list(distant)[halved:], take_and_add, acc)

    def scatter_direct(which, part_buf, in_buf, part, halved, relay_buf=None, hop=0, bit=None, base=None):
        count = part_buf.shape[1]
        half = count // 2 if hop else count
        rows = block_of(bit, half) if hop else pl.ds(0, half)
        other_rows = block_of(1 - bit, half) if hop else rows

        def go(slot, stand_in, times=1):
            semaphore_slot = slot if stand_in >= half_panels else stand_in
            if hop:
                ship(part_buf.at[slot, other_rows], in_buf.at[1, slot], which, 1, semaphore_slot, hop, at(slot), times)
            if stand_in:
                ship(part_buf.at[slot, rows], in_buf.at[0, slot], which, 0, semaphore_slot, 0, at(slot), times)

        def fill(slot):
            part_buf[slot] = part(at(slot))

        def fill_and_go(slot, stand_in, times, carry):
            fill(slot)
            go(slot, stand_in, times)
            return carry

        def fill_and_relay(slot, stand_in, times, carry):
            fill(half_panels + slot)
            ship(part_buf.at[half_panels + slot], relay_buf.at[slot], which, 2, stand_in, 0, at(slot), times)
            return carry

        if halved:
            walk(list(near)[::-1], fill_and_relay, 0)
        else:
            walk([half_panels ^ i for i in FAR_ORDER if i < half_panels], fill_and_go, 0)
        walk(list(near)[::-1], fill_and_go, 0)
        own = part(at(0))
        if hop:
            part_buf[0] = base[...] - own
            go(0, 0)
        else:
            own = own if base is None else base[...] - own
        if halved:
            fill(half_panels)
        yield
        if halved:
            total = part_buf[half_panels]
            landed(relay_buf.at[pl.ds(1, half_panels - 1)], which, 2, 0)
            for slot in near:
                total = total + relay_buf[slot]
            part_buf[half_panels] = total
            go(half_panels, half_panels)
            yield
        sources = [half_panels] if halved else list(distant)
        sign = 1 if base is None else -1
        acc = part_buf[0, rows, :] if hop else own
        landed(in_buf.at[0, pl.ds(1, half_panels - 1)], which, 0, 0)
        for slot in near:
            acc = acc + sign * in_buf[0, slot]
        for slot in sources:
            landed(in_buf.at[0, slot], which, 0, slot)
            acc = acc + sign * in_buf[0, slot]
        if not hop:
            return acc
        landed(in_buf.at[1, pl.ds(0, half_panels)], which, 1, 0)
        there = in_buf[1, 0]
        for slot in near:
            there = there - in_buf[1, slot]
        for slot in sources:
            landed(in_buf.at[1, slot], which, 1, slot)
            there = there - in_buf[1, slot]
        return acc, there

    def gather(which, buf, value, use, acc):
        buf[0] = value
        for d in far_order:
            to_row(buf.at[0], buf.at[d * inner], which, d * inner, d).start()

        def forward(d):
            def go(e, _):
                to_col(buf.at[d * inner], buf.at[d * inner + e], which, d * inner + e, e).start()
                return _
            loop(1, inner, go, 0)

        def arrived(d, acc):
            def go(e, acc):
                slot = d * inner + e
                to_col(buf.at[slot], buf.at[slot], which, slot, e).wait_recv()
                return use(acc, buf[slot], place(d, e))
            return loop(1, inner, go, acc)

        forward(0)
        acc = use(acc, buf[0], place(0, 0))
        yield
        last = 0
        for d in row_order:
            to_row(buf.at[d * inner], buf.at[d * inner], which, d * inner, d).wait_recv()
            forward(d)
            acc = use(acc, buf[d * inner], place(d, 0))
            acc = arrived(last, acc)
            last = d
        yield
        return arrived(last, acc)

    def scatter(which, part_buf, in_buf, part):
        for d in far_order + [0]:
            def go(e, _, d=d):
                slot = d * inner + e
                part_buf[slot] = part(place(d, e))
                to_col(part_buf.at[slot], in_buf.at[slot], which, slot, e).start()
                return _
            loop(1, inner, go, 0)

        yield

        def collect(d):
            def go(e, acc):
                slot = d * inner + e
                to_col(in_buf.at[slot], in_buf.at[slot], which, slot, e).wait_recv()
                return acc + in_buf[slot]
            return loop(1, inner, go, part(place(d, 0)))

        for d in far_order:
            slot = d * inner
            part_buf[slot] = collect(d)
            to_row(part_buf.at[slot], in_buf.at[slot], which, slot, d).start()
        acc = collect(0)
        yield
        for d in row_order:
            slot = d * inner
            to_row(in_buf.at[slot], in_buf.at[slot], which, slot, d).wait_recv()
            acc = acc + in_buf[slot]
        return acc

    def swap(source, target, which, level):
        return pltpu.make_async_remote_copy(
            src_ref=source, dst_ref=target, send_sem=ref[SWAP_SEND_SEM].at[which[0], which[1]],
            recv_sem=ref[SWAP_RECV_SEM].at[which[0], which[1]], device_id={LEAF_AXIS: leaf ^ (1 << level)},
            device_id_type=MESH)

    swaps = []

    def begin_swap(level, batch):
        count = counts[level]
        copy = swap(ref[CURRENT, level, batch].at[block_of(1 - bits[level], count)],
                    ref[SWAPPED, level, batch], (batch, level), level)
        copy.start()
        swaps.append(copy)
        return copy

    def spread(level, side, value):
        if merged:
            return dot(split(value), ref[TABLES_T][level, side], NN)
        return dot(split(value), tables[level, side], NT)

    def run(batch):
        vertical = None
        for level in range(levels):
            count = counts[level]
            top = level == 0
            current = ref[CURRENT, level, batch]
            if merged and not top:
                mine, other = vertical
                total = spread(level, 0, mine) + spread(level, 1, other)
            else:
                copy = begin_swap(level, batch)
                yield
                total = spread(level, 0, current[block_of(bits[level], count), :])
                copy.wait_recv()
                total = total + spread(level, 1, ref[SWAPPED, level, batch][...])
            assembled = fold(total)
            kept = ref[KEPT, level, batch]
            kept[...] = assembled[:, pivot_block:]
            if not merged:
                ready(2 * level)

            def use(acc, value, index, level=level):
                if merged:
                    return acc + dot(split(value), ref[PIVOTS_T][level, block_of(index, pivot_block), :], NN)
                return acc + dot(split(value), pivots[level, :, block_of(index, pivot_block)], NT)

            which = 2 * level
            value = ref[RHS, level, batch][...] + assembled[:, :pivot_block]
            zero = jnp.zeros((2 * count, pivot_block), jnp.float32)
            if merged:
                solved = yield from gather_direct(
                    (batch, which), ref[GATHER, which, batch], value, use, zero, level < levels - 1,
                    prepare=functools.partial(ready, 2 * level))
            else:
                solved = yield from gather((batch, which), ref[GATHER, which, batch], value, use, zero)
            solved = fold(solved)
            ref[SOLVED, level, batch][...] = solved
            pair = ref[PAIR, level, batch]
            pair[...] = split(solved)
            ready(2 * level + 1)

            def part(index, level=level, pair=pair):
                if merged:
                    return fold(dot(pair[...], ref[UPDATES_T][level, :, block_of(index, update_block)], NN))
                return fold(dot(pair[...], updates[level, block_of(index, update_block), :], NT))

            which = 2 * level + 1
            buffers = ref[PART, which, batch], ref[LAND, which, batch]
            last = level == levels - 1
            if not merged:
                coupled = yield from scatter((batch, which), *buffers, part)
                ref[CURRENT, level + 1, batch][...] = kept[...] - coupled
            elif last:
                vertical = yield from scatter_direct((batch, which), *buffers, part, level < levels - 1, ref[RELAY, which, batch], base=kept)
            else:
                vertical = yield from scatter_direct(
                    (batch, which), *buffers, part, level < levels - 1, ref[RELAY, which, batch],
                    1 << (level + 1), bits[level + 1], kept)

        if not merged:
            ready(2 * levels)
        count = counts[levels - 1]

        def use_root(acc, value, index):
            if merged:
                return acc + dot(split(value), ref[ROOT_T][block_of(index, update_block), :], NN)
            return acc + dot(split(value), root[:, block_of(index, update_block)], NT)

        zero = jnp.zeros((2 * count, update_block), jnp.float32)
        buf = ref[GATHER, 2 * levels, batch]
        if merged:
            known = yield from gather_direct((batch, 2 * levels), buf, vertical, use_root, zero, False, prepare=functools.partial(ready, 2 * levels))
        else:
            known = yield from gather((batch, 2 * levels), buf, ref[CURRENT, levels, batch][...], use_root, zero)
        ref[KNOWN, levels, batch][...] = fold(known)

        for level in range(levels - 1, -1, -1):
            count = counts[level]
            top = level == 0
            last = level == levels - 1
            which = 2 * levels + 1 + 2 * level

            def use(acc, value, index, level=level):
                return acc + dot(split(value), updates[level, block_of(index, update_block), :], NN)

            zero = jnp.zeros((2 * count, pivot_block), jnp.float32)
            buf = ref[GATHER, which, batch]
            if not merged:
                known = ref[KNOWN, level + 1, batch]
                coupling = yield from gather((batch, which), buf, known[...], use, zero)
            elif last:
                coupling = yield from gather_direct(
                    (batch, which), buf, ref[KNOWN, levels, batch][...], use, zero, level < levels - 1)
            else:
                coupling = yield from gather_direct(
                    (batch, which), buf, None, use, zero, level < levels - 1, 1 << (level + 1),
                    ref[CHILD, level + 1, batch], bits[level + 1])
            coupling = fold(coupling)
            pair = ref[PAIR, level, batch]
            pair[...] = split(ref[SOLVED, level, batch][...] - coupling)

            def part(index, level=level, pair=pair):
                return fold(dot(pair[...], pivots[level, :, block_of(index, pivot_block)], NN))

            which = which + 1
            buffers = ref[PART, which, batch], ref[LAND, which, batch]
            if merged:
                own = yield from scatter_direct(
                    (batch, which), *buffers, part, level < levels - 1, ref[RELAY, which, batch])
                known = ref[GATHER, which - 1, batch][0]
            else:
                own = yield from scatter((batch, which), *buffers, part)
                known = ref[KNOWN, level + 1, batch][...]
            own_pair, known_pair = split(own), split(known)

            def child(side):
                return fold(dot(own_pair, tables[level, side, :pivot_block, :], NN)
                            + dot(known_pair, tables[level, side, pivot_block:, :], NN))

            ref[CHILD, level, batch][...] = child(1)
            rows = block_of(bits[level], count)
            exchange = top or not merged
            if exchange:
                copy = swap(ref[CHILD, level, batch], ref[KNOWN, level, batch].at[rows], (batch, 1 if merged else levels + level), level)
                copy.start()
                swaps.append(copy)
                ref[KNOWN, level, batch][rows, :] = child(0)
            else:
                ref[GATHER, 2 * levels + 1 + 2 * (level - 1), batch][0, rows, :] = child(0)
            ref[OWN, level, batch][...] = own
            size = levels - 1 - level

            def emit(level=level, count=count, size=size):
                for g in range(1 << size):
                    for k in range(group):
                        pivot_out[0, pl.ds(offsets[level] + batch * count + (k << size | bit_reverse(g, size)), 1), :] = (
                            ref[OWN, level, batch][pl.ds(g * group + k, 1), :])
            emits.append(emit)
            if exchange:
                emit_all()
                yield
                copy.wait_recv()

        known = ref[KNOWN, 0, batch]
        for g in range(1 << levels):
            for k in range(group):
                update_out[0, pl.ds(batch * vectors + (k << levels | bit_reverse(g, levels)), 1), :] = known[pl.ds(g * group + k, 1), :]

    emits = []

    def emit_all():
        while emits:
            emits.pop()()

    runs = [run(batch) for batch in range(batches)]
    for one in runs:
        next(one)
    for level in range(1, levels):
        build(level)
    turns = list(TURNS)
    while runs:
        runs = [one for one in runs if next(one, True) is None]
        if merged and turns:
            turn_some(turns.pop(0))

    for copy in swaps:
        copy.wait_send()
    tally = ref[TALLY]
    for which, count in sent.items():
        hand(tally.at[pl.ds(0, count)], tally.at[pl.ds(0, count)], which, 0, 1, {PANEL_AXIS: panel ^ 1}).wait_send()
    for which in range(0 if merged else 4 * levels + 1):
        for batch in range(batches):
            name = (GATHER, which, batch)
            buf = ref[name] if name in ref else ref[PART, which, batch]

            def finish(slot, _, which=which, batch=batch, buf=buf):
                send(buf.at[slot], buf.at[slot], (batch, which), slot, {PANEL_AXIS: panel ^ 1}).wait_send()
                return _
            lax.fori_loop(1, panels, finish, 0)


def hand_over(pivot_in, update_in, pivot_out, update_out):
    update_out[...] = update_in[...]
    pivot_out[...] = pivot_in[...]


def local(panels, pivot_rhs, subtree_update, lower_pivot, lower_update, row_map, root_inverse):
    levels = lower_pivot.shape[0]
    pivot_block, update_block = pivot_rhs.shape[2], subtree_update.shape[2]
    batches = BATCHES if subtree_update.shape[1] >> levels >= 8 * BATCHES else 1
    vectors = subtree_update.shape[1] // batches
    outer = min(OUTER_MAX, panels)
    inner = panels // outer
    slots = pivot_block + update_block
    merged = panels <= DIRECT_PANELS
    whole_rows = vectors // 2
    f32, bf16 = jnp.float32, jnp.bfloat16
    scratch = {
        PIVOTS: pltpu.VMEM((levels,) + lower_pivot.shape[2:], bf16),
        UPDATES: pltpu.VMEM((levels,) + lower_update.shape[2:], bf16),
        ROOT: pltpu.VMEM(root_inverse.shape, bf16),
        TABLES: pltpu.VMEM((levels, 2, slots, update_block), bf16),
    }
    if merged:
        scratch[TABLES_T] = pltpu.VMEM((levels, 2, update_block, slots), bf16)
        scratch[PIVOTS_T] = pltpu.VMEM((levels, lower_pivot.shape[3], pivot_block), bf16)
        scratch[UPDATES_T] = pltpu.VMEM((levels, pivot_block, lower_update.shape[2]), bf16)
        scratch[ROOT_T] = pltpu.VMEM((root_inverse.shape[1], update_block), bf16)
    for batch in range(batches):
        for level in range(levels):
            count = vectors >> (level + 1)
            back = 2 * levels + 1 + 2 * level
            scratch[CURRENT, level, batch] = pltpu.VMEM((2 * count, update_block), f32)
            scratch[KNOWN, level, batch] = pltpu.VMEM((2 * count, update_block), f32)
            scratch[SWAPPED, level, batch] = pltpu.VMEM((count, update_block), f32)
            scratch[CHILD, level, batch] = pltpu.VMEM((count, update_block), f32)
            scratch[KEPT, level, batch] = pltpu.VMEM((count, update_block), f32)
            scratch[SOLVED, level, batch] = pltpu.VMEM((count, pivot_block), f32)
            scratch[RHS, level, batch] = pltpu.VMEM((count, pivot_block), f32)
            scratch[OWN, level, batch] = pltpu.VMEM((count, pivot_block), f32)
            scratch[PAIR, level, batch] = pltpu.VMEM((2 * count, pivot_block), bf16)
            scratch[GATHER, 2 * level, batch] = pltpu.VMEM((panels, count, pivot_block), f32)
            scratch[GATHER, back, batch] = pltpu.VMEM((panels, count, update_block), f32)
            for which, width in ((2 * level + 1, update_block), (back + 1, pivot_block)):
                scratch[PART, which, batch] = pltpu.VMEM((panels, count, width), f32)
                if not merged:
                    scratch[LAND, which, batch] = pltpu.VMEM((panels, count, width), f32)
                elif which == 2 * level + 1 and level < levels - 1:
                    scratch[LAND, which, batch] = pltpu.VMEM((2, panels, count // 2, width), f32)
                else:
                    scratch[LAND, which, batch] = pltpu.VMEM((1, panels, count, width), f32)
                if merged:
                    scratch[RELAY, which, batch] = pltpu.VMEM((panels // 2, count, width), f32)
        count = vectors >> levels
        scratch[CURRENT, levels, batch] = pltpu.VMEM((count, update_block), f32)
        scratch[KNOWN, levels, batch] = pltpu.VMEM((count, update_block), f32)
        scratch[GATHER, 2 * levels, batch] = pltpu.VMEM((panels, count, update_block), f32)
    if merged:
        scratch[SEND_SEM] = pltpu.SemaphoreType.DMA((batches, 4 * levels + 1))
        scratch[RECV_SEM] = pltpu.SemaphoreType.DMA((batches, 2, 2 + panels // 2))
        scratch[CROSS_SEM] = pltpu.SemaphoreType.DMA((batches, max(1, 2 * levels - 2), 2))
    else:
        scratch[SEND_SEM] = pltpu.SemaphoreType.DMA((batches, 4 * levels + 1, panels))
        scratch[RECV_SEM] = pltpu.SemaphoreType.DMA((batches, 4 * levels + 1, panels))
    scratch[MAPS] = pltpu.VMEM(row_map.shape, jnp.int32)
    scratch[UPDATE_IN] = pltpu.VMEM(subtree_update.shape, f32)
    scratch[PIVOT_IN] = pltpu.VMEM(pivot_rhs.shape, f32)
    scratch[TALLY] = pltpu.VMEM((panels * whole_rows if merged else 8, update_block), f32)
    scratch[SWAP_SEND_SEM] = pltpu.SemaphoreType.DMA((batches, 2 if merged else 2 * levels))
    scratch[SWAP_RECV_SEM] = pltpu.SemaphoreType.DMA((batches, 2 if merged else 2 * levels))
    scratch[LOAD_SEM] = pltpu.SemaphoreType.DMA((2 * levels + 4,))
    names = [PIVOT_RHS, SUBTREE_UPDATE, ROW_MAP, LOWER_PIVOT, LOWER_UPDATE, ROOT_INVERSE,
             PIVOT_SOLUTION, SUBTREE_SOLUTION] + list(scratch)
    vmem, anywhere = pl.BlockSpec(memory_space=pltpu.VMEM), pl.BlockSpec(memory_space=pl.ANY)
    results = pl.pallas_call(
        functools.partial(kernel, levels, batches, outer, inner, names),
        out_shape=(jax.ShapeDtypeStruct(pivot_rhs.shape, f32),
                   jax.ShapeDtypeStruct(subtree_update.shape, f32)),
        in_specs=[anywhere] * 6,
        out_specs=(vmem, vmem),
        scratch_shapes=list(scratch.values()),
        compiler_params=pltpu.CompilerParams(collective_id=0, has_side_effects=True, vmem_limit_bytes=VMEM_LIMIT),
    )(pivot_rhs, subtree_update, row_map, lower_pivot, lower_update, root_inverse)
    return pl.pallas_call(
        hand_over,
        out_shape=tuple(jax.ShapeDtypeStruct(one.shape, f32) for one in results),
        in_specs=[vmem] * 2,
        out_specs=(vmem, vmem),
    )(*results)


def solution(mesh):
    in_specs = (
        P(LEAF_AXIS, None, PANEL_AXIS),
        P(LEAF_AXIS, None, PANEL_AXIS),
        P(None, LEAF_AXIS, PANEL_AXIS, None),
        P(None, LEAF_AXIS, None, PANEL_AXIS),
        P(None, LEAF_AXIS, None, PANEL_AXIS),
        P(PANEL_AXIS, None),
    )
    out_specs = (P(LEAF_AXIS, None, PANEL_AXIS), P(LEAF_AXIS, None, PANEL_AXIS))
    return jax.shard_map(functools.partial(local, mesh.shape[PANEL_AXIS]), mesh=mesh, in_specs=in_specs,
                         out_specs=out_specs, check_vma=False)
```
